32 devices in a mesh: dp: 16 (over z, y, core), tensor: 2 (over x).
Axes of the slice: x: 2, y: 2, z: 4, core: 2. Of those that a mesh axis runs over, the one named last changes fastest.
Arguments:
- hidden_in: float32 [16384, 768], P(('dp', 'tensor')), may hold values from -6 to 6
- cotangent: float32 [16384, 768], P(('dp', 'tensor')), may hold values from -6 to 6
- proj_zx: float32 [768, 2, 1536], P('dp', None, 'tensor'), may hold values from -0.21875 to 0.21875
- proj_dt: float32 [768, 24], P('dp', 'tensor'), may hold values from -0.21875 to 0.21875
- proj_bc: float32 [768, 256], P('dp'), may hold values from -0.21875 to 0.21875
- proj_out: float32 [768, 1536], P('dp', 'tensor'), may hold values from -0.15625 to 0.15625
- norm_gain: float32 [768], replicated, may hold values from 0.5 to 1.5
- conv_inner: float32 [5, 1536], P(None, 'tensor'), may hold values from -0.5 to 0.5
- conv_shared: float32 [5, 256], replicated, may hold values from -0.5 to 0.5
- head_table: float32 [3, 24], P(None, 'tensor'), may hold values from -7 to 3, as said below
- gate_gain: float32 [1536], P('tensor'), may hold values from 0.5 to 1.5
- mom_zx: float32 [768, 2, 1536], P('dp', None, 'tensor'), may hold values from -76.8 to 76.8
- mom_dt: float32 [768, 24], P('dp', 'tensor'), may hold values from -76.8 to 76.8
- mom_bc: float32 [768, 256], P('dp'), may hold values from -76.8 to 76.8
- mom_out: float32 [768, 1536], P('dp', 'tensor'), may hold values from -76.8 to 76.8
- mom_norm: float32 [768], replicated, may hold values from -76.8 to 76.8
- mom_conv: float32 [5, 1536], P(None, 'tensor'), may hold values from -76.8 to 76.8
- mom_shared: float32 [5, 256], replicated, may hold values from -76.8 to 76.8
- mom_head: float32 [3, 24], P(None, 'tensor'), may hold values from -76.8 to 76.8
- mom_gate: float32 [1536], P('tensor'), may hold values from -76.8 to 76.8
- var_zx: float32 [768, 2, 1536], P('dp', None, 'tensor'), may hold values from 16.384 to 1638.4
- var_dt: float32 [768, 24], P('dp', 'tensor'), may hold values from 16.384 to 1638.4
- var_bc: float32 [768, 256], P('dp'), may hold values from 16.384 to 1638.4
- var_out: float32 [768, 1536], P('dp', 'tensor'), may hold values from 16.384 to 1638.4
- var_norm: float32 [768], replicated, may hold values from 16.384 to 1638.4
- var_conv: float32 [5, 1536], P(None, 'tensor'), may hold values from 16.384 to 1638.4
- var_shared: float32 [5, 256], replicated, may hold values from 16.384 to 1638.4
- var_head: float32 [3, 24], P(None, 'tensor'), may hold values from 16.384 to 1638.4
- var_gate: float32 [1536], P('tensor'), may hold values from 16.384 to 1638.4
Outputs:
- hidden_out: float32 [16384, 768], P(('dp', 'tensor'))
- grad_hidden: float32 [16384, 768], P(('dp', 'tensor'))
- grad_zx: float32 [768, 2, 1536], P('dp', None, 'tensor')
- grad_dt: float32 [768, 24], P('dp', 'tensor')
- grad_bc: float32 [768, 256], P('dp')
- grad_out: float32 [768, 1536], P('dp', 'tensor')
- grad_norm: float32 [768], replicated
- grad_conv: float32 [5, 1536], P(None, 'tensor')
- grad_shared: float32 [5, 256], replicated
- grad_head: float32 [3, 24], P(None, 'tensor')
- grad_gate: float32 [1536], P('tensor')
- new_zx: float32 [768, 2, 1536], P('dp', None, 'tensor')
- new_dt: float32 [768, 24], P('dp', 'tensor')
- new_bc: float32 [768, 256], P('dp')
- new_out: float32 [768, 1536], P('dp', 'tensor')
- new_norm: float32 [768], replicated
- new_conv: float32 [5, 1536], P(None, 'tensor')
- new_shared: float32 [5, 256], replicated
- new_head: float32 [3, 24], P(None, 'tensor')
- new_gate: float32 [1536], P('tensor')
- new_mom_zx: float32 [768, 2, 1536], P('dp', None, 'tensor')
- new_mom_dt: float32 [768, 24], P('dp', 'tensor')
- new_mom_bc: float32 [768, 256], P('dp')
- new_mom_out: float32 [768, 1536], P('dp', 'tensor')
- new_mom_norm: float32 [768], replicated
- new_mom_conv: float32 [5, 1536], P(None, 'tensor')
- new_mom_shared: float32 [5, 256], replicated
- new_mom_head: float32 [3, 24], P(None, 'tensor')
- new_mom_gate: float32 [1536], P('tensor')
- new_var_zx: float32 [768, 2, 1536], P('dp', None, 'tensor')
- new_var_dt: float32 [768, 24], P('dp', 'tensor')
- new_var_bc: float32 [768, 256], P('dp')
- new_var_out: float32 [768, 1536], P('dp', 'tensor')
- new_var_norm: float32 [768], replicated
- new_var_conv: float32 [5, 1536], P(None, 'tensor')
- new_var_shared: float32 [5, 256], replicated
- new_var_head: float32 [3, 24], P(None, 'tensor')
- new_var_gate: float32 [1536], P('tensor')
The draws below stay inside these ranges and needn't reach their ends.
Inputs may be any that keep to these rules, and one draw needn't show every extreme that they name: `head_table`: row 0 holds step size offsets, row 1 logarithms of decay rates, row 2 skip gains.
All inputs are finite; a program needn't handle non-finite values.
Results may differ from the reference program's by a relative error of at most 0.0033.
The reference program's roundings to bfloat16 on the way (of `normed`, `normed_gate` and `cot16`) count: a program that leaves them out, or rounds other values in their place, can miss the bound.
Values may be sent and summed in bfloat16 or wider, within the bound.
A program may use at most 192 MiB of HBM per device.

```python
import math
import jax
import jax.numpy as jnp
from jax import lax

D = 768
HEADS = 24
HEAD_DIM = 64
STATE = 128
CONV_WIDTH = 4
SPAN = 256
LEN = 512
STEP = 3
INNER = 1536
TOKENS = 16384


def draw_head_table(key, part):
    first, second, third = jax.random.split(key, 3)
    step_size = jnp.exp(jax.random.uniform(first, (HEADS,), jnp.float32, jnp.log(0.001), jnp.log(0.1)))
    rate_log = jnp.log(jax.random.uniform(second, (HEADS,), jnp.float32, 1.0, 16.0))
    offset = jnp.log(jnp.expm1(step_size))
    skip_gain = jax.random.uniform(third, (HEADS,), jnp.float32, 0.5, 1.5)
    return jnp.stack([offset, rate_log, skip_gain], axis=0)


def shard_levels(rng, dims, pieces, smallest, largest):
    gain, own = 1.0, jax.random.fold_in(rng, 6)
    for axis_at, blocks in pieces:
        heights = jnp.exp(jax.random.uniform(jax.random.fold_in(own, axis_at), (blocks,), jnp.float32, smallest / len(pieces), largest / len(pieces)))
        gain = gain * jnp.repeat(heights, dims[axis_at] // blocks).reshape([-1 if axis == axis_at else 1 for axis in range(len(dims))])
    return gain


def centred(key, dims, scale, reach, shards=(), kind=jnp.bfloat16):
    values = scale * jax.random.normal(key, dims, jnp.float32)
    if shards:
        values = values * shard_levels(key, dims, shards, -0.22, 0.18)
    return jnp.clip(values, -reach, reach).astype(kind)


def setup_inputs(seed: int = 0) -> dict:
    key_of = jax.random.split(jax.random.key(seed), 30)
    hidden_in = centred(key_of[0], (TOKENS, D), 1.0, 6.0, ((0, 32),), jnp.float32)
    cotangent = centred(key_of[1], (TOKENS, D), 1.0, 6.0, ((0, 32),), jnp.float32)
    proj_zx = centred(key_of[2], (D, 2, INNER), D ** -0.5, 0.21875, ((0, 16), (2, 2)), jnp.float32)
    proj_dt = centred(key_of[3], (D, HEADS), D ** -0.5, 0.21875, ((0, 16), (1, 2)), jnp.float32)
    proj_bc = centred(key_of[4], (D, 2 * STATE), D ** -0.5, 0.21875, ((0, 16),), jnp.float32)
    proj_out = centred(key_of[5], (D, INNER), INNER ** -0.5, 0.15625, ((0, 16), (1, 2)), jnp.float32)
    norm_gain = jnp.clip(1.0 + 0.1 * jax.random.normal(key_of[6], (D,), jnp.float32), 0.5, 1.5)
    conv_inner = jnp.clip(jax.random.uniform(key_of[7], (CONV_WIDTH + 1, INNER), jnp.float32, -0.5, 0.5) * shard_levels(key_of[7], (CONV_WIDTH + 1, INNER), ((1, 2),), -0.4, 0.0), -0.5, 0.5)
    conv_shared = jnp.clip(jax.random.uniform(key_of[8], (CONV_WIDTH + 1, 2 * STATE), jnp.float32, -0.5, 0.5), -0.5, 0.5)
    head_table = draw_head_table(jax.random.fold_in(key_of[29], 71), 0)
    gate_gain = jnp.clip(1.0 + 0.1 * jax.random.normal(key_of[10], (INNER,), jnp.float32), 0.5, 1.5)
    mom_zx = centred(key_of[11], (D, 2, INNER), (0.1 * TOKENS ** 0.5), 76.8, ((0, 16), (2, 2)), jnp.float32)
    mom_dt = centred(key_of[12], (D, HEADS), (0.1 * TOKENS ** 0.5), 76.8, ((0, 16), (1, 2)), jnp.float32)
    mom_bc = centred(key_of[13], (D, 2 * STATE), (0.1 * TOKENS ** 0.5), 76.8, ((0, 16),), jnp.float32)
    mom_out = centred(key_of[14], (D, INNER), (0.1 * TOKENS ** 0.5), 76.8, ((0, 16), (1, 2)), jnp.float32)
    mom_norm = centred(key_of[15], (D,), (0.1 * TOKENS ** 0.5), 76.8, (), jnp.float32)
    mom_conv = centred(key_of[16], (CONV_WIDTH + 1, INNER), (0.1 * TOKENS ** 0.5), 76.8, ((1, 2),), jnp.float32)
    mom_shared = centred(key_of[17], (CONV_WIDTH + 1, 2 * STATE), (0.1 * TOKENS ** 0.5), 76.8, (), jnp.float32)
    mom_head = centred(key_of[18], (3, HEADS), (0.1 * TOKENS ** 0.5), 76.8, ((1, 2),), jnp.float32)
    mom_gate = centred(key_of[19], (INNER,), (0.1 * TOKENS ** 0.5), 76.8, ((0, 2),), jnp.float32)
    var_zx = jnp.clip(jnp.exp(math.log(1638.4) - 4.6051702 * jax.random.uniform(key_of[20], (D, 2, INNER), jnp.float32) ** shard_levels(key_of[20], (D, 2, INNER), ((0, 16), (2, 2)), -0.2, 0.2)), 16.384, 1638.4)
    var_dt = jnp.clip(jnp.exp(math.log(1638.4) - 4.6051702 * jax.random.uniform(key_of[21], (D, HEADS), jnp.float32) ** shard_levels(key_of[21], (D, HEADS), ((0, 16), (1, 2)), -0.2, 0.2)), 16.384, 1638.4)
    var_bc = jnp.clip(jnp.exp(math.log(1638.4) - 4.6051702 * jax.random.uniform(key_of[22], (D, 2 * STATE), jnp.float32) ** shard_levels(key_of[22], (D, 2 * STATE), ((0, 16),), -0.2, 0.2)), 16.384, 1638.4)
    var_out = jnp.clip(jnp.exp(math.log(1638.4) - 4.6051702 * jax.random.uniform(key_of[23], (D, INNER), jnp.float32) ** shard_levels(key_of[23], (D, INNER), ((0, 16), (1, 2)), -0.2, 0.2)), 16.384, 1638.4)
    var_norm = jnp.clip(jnp.exp(jax.random.uniform(key_of[24], (D,), jnp.float32, math.log(16.384), math.log(1638.4))), 16.384, 1638.4)
    var_conv = jnp.clip(jnp.exp(math.log(1638.4) - 4.6051702 * jax.random.uniform(key_of[25], (CONV_WIDTH + 1, INNER), jnp.float32) ** shard_levels(key_of[25], (CONV_WIDTH + 1, INNER), ((1, 2),), -0.2, 0.2)), 16.384, 1638.4)
    var_shared = jnp.clip(jnp.exp(jax.random.uniform(key_of[26], (CONV_WIDTH + 1, 2 * STATE), jnp.float32, math.log(16.384), math.log(1638.4))), 16.384, 1638.4)
    var_head = jnp.clip(jnp.exp(math.log(1638.4) - 4.6051702 * jax.random.uniform(key_of[27], (3, HEADS), jnp.float32) ** shard_levels(key_of[27], (3, HEADS), ((1, 2),), -0.2, 0.2)), 16.384, 1638.4)
    var_gate = jnp.clip(jnp.exp(math.log(1638.4) - 4.6051702 * jax.random.uniform(key_of[28], (INNER,), jnp.float32) ** shard_levels(key_of[28], (INNER,), ((0, 2),), -0.2, 0.2)), 16.384, 1638.4)
    return {"hidden_in": hidden_in, "cotangent": cotangent, "proj_zx": proj_zx, "proj_dt": proj_dt, "proj_bc": proj_bc, "proj_out": proj_out, "norm_gain": norm_gain, "conv_inner": conv_inner, "conv_shared": conv_shared, "head_table": head_table, "gate_gain": gate_gain, "mom_zx": mom_zx, "mom_dt": mom_dt, "mom_bc": mom_bc, "mom_out": mom_out, "mom_norm": mom_norm, "mom_conv": mom_conv, "mom_shared": mom_shared, "mom_head": mom_head, "mom_gate": mom_gate, "var_zx": var_zx, "var_dt": var_dt, "var_bc": var_bc, "var_out": var_out, "var_norm": var_norm, "var_conv": var_conv, "var_shared": var_shared, "var_head": var_head, "var_gate": var_gate}


epsilon = 1e-05
precise = lax.Precision.HIGHEST
beta_first = 0.9
beta_second = 0.95
learn_rate = 0.1
weight_decay = 0.01
adam_epsilon = 1e-08

def conv_silu(values, kernel, seq_count):
    kernel_taps = kernel.shape[0] - 1
    shaped = values.reshape(seq_count, LEN, values.shape[1])
    padded = jnp.pad(shaped, ((0, 0), (kernel_taps - 1, 0), (0, 0)))
    summed = kernel[kernel_taps] + jnp.zeros_like(shaped)
    for offset in range(kernel_taps):
        summed = summed + kernel[offset] * padded[:, offset:offset + LEN]
    return jax.nn.silu(summed).reshape(values.shape)

def state_space(values, step_size, decay_rate, key_rows, query_rows):
    seq_count = values.shape[0] // LEN
    blocks = LEN // SPAN
    head_count = step_size.shape[1]
    state_dim = key_rows.shape[1]
    block_x = values.reshape(seq_count, blocks, SPAN, head_count, HEAD_DIM)
    block_dt = step_size.reshape(seq_count, blocks, SPAN, head_count)
    block_b = key_rows.reshape(seq_count, blocks, SPAN, state_dim)
    block_c = query_rows.reshape(seq_count, blocks, SPAN, state_dim)
    cumul = jnp.cumsum(block_dt * decay_rate, axis=2)
    position = jnp.arange(SPAN)
    lower_mask = (position[:, None] >= position[None, :])[:, :, None]
    spread = cumul[:, :, :, None, :] - cumul[:, :, None, :, :]
    within = jnp.where(lower_mask, jnp.exp(jnp.where(lower_mask, spread, 0.0)), 0.0)
    scores = jnp.einsum('bcin,bcjn->bcij', block_c, block_b, precision=precise)
    weighted = block_x * block_dt[..., None]
    mixing_table = scores[..., None] * within
    diag_part = jnp.einsum('bcijh,bcjhp->bcihp', mixing_table, weighted, precision=precise)
    to_end = jnp.exp(cumul[:, :, -1:, :] - cumul)
    states = jnp.einsum('bcjn,bcjhp->bchpn', block_b, to_end[..., None] * weighted, precision=precise)
    whole_decay = jnp.exp(cumul[:, :, -1, :])

    def advance(running, inputs):
        block_state, block_decay = inputs
        return (running * block_decay[:, :, None, None] + block_state, running)
    zero_state = jnp.zeros((seq_count, head_count, HEAD_DIM, state_dim), jnp.float32)
    final_state, entering = lax.scan(advance, zero_state, (jnp.moveaxis(states, 1, 0), jnp.moveaxis(whole_decay, 1, 0)))
    entering = jnp.moveaxis(entering, 0, 1)
    off_part = jnp.einsum('bcin,bchpn->bcihp', block_c, entering, precision=precise) * jnp.exp(cumul)[..., None]
    return (diag_part + off_part).reshape(seq_count * LEN, head_count * HEAD_DIM)

def mixing(x_raw, bc_raw, dt_raw, conv_inner, conv_shared, head_table):
    seq_count = x_raw.shape[0] // LEN
    x_conv = conv_silu(x_raw, conv_inner, seq_count)
    bc_conv = conv_silu(bc_raw, conv_shared, seq_count)
    state_dim = bc_raw.shape[1] // 2
    step_size = jax.nn.softplus(dt_raw + head_table[0])
    decay_rate = -jnp.exp(head_table[1])
    result = state_space(x_conv, step_size, decay_rate, bc_conv[:, :state_dim], bc_conv[:, state_dim:])
    return result + jnp.repeat(head_table[2], HEAD_DIM) * x_conv

def adam_update(weight, moment, second, gradient):
    moment_new = beta_first * moment + (1.0 - beta_first) * gradient
    second_new = beta_second * second + (1.0 - beta_second) * gradient * gradient
    corr_first = 1.0 - beta_first ** STEP
    corr_second = 1.0 - beta_second ** STEP
    update = moment_new / corr_first / (jnp.sqrt(second_new / corr_second) + adam_epsilon)
    return (weight - learn_rate * (update + weight_decay * weight), moment_new, second_new)

def reference(hidden_in, cotangent, proj_zx, proj_dt, proj_bc, proj_out, norm_gain, conv_inner, conv_shared, head_table, gate_gain, mom_zx, mom_dt, mom_bc, mom_out, mom_norm, mom_conv, mom_shared, mom_head, mom_gate, var_zx, var_dt, var_bc, var_out, var_norm, var_conv, var_shared, var_head, var_gate):
    flat_zx = proj_zx.astype(jnp.bfloat16).reshape(D, 2 * INNER)
    weight_dt = proj_dt.astype(jnp.bfloat16)
    weight_bc = proj_bc.astype(jnp.bfloat16)
    weight_out = proj_out.astype(jnp.bfloat16)
    seq_count = hidden_in.shape[0] // LEN

    def one_sequence(totals, inputs):
        rows_in, cot_rows = inputs
        scale_in = lax.rsqrt(lax.optimization_barrier(jnp.mean(rows_in * rows_in, axis=-1, keepdims=True)) + epsilon)
        unit_in = rows_in * scale_in
        normed = (unit_in * norm_gain).astype(jnp.bfloat16)
        zx_raw = jnp.dot(normed, flat_zx, preferred_element_type=jnp.float32)
        gate_pre = zx_raw[:, :INNER]
        x_raw = zx_raw[:, INNER:]
        bc_raw = jnp.dot(normed, weight_bc, preferred_element_type=jnp.float32)
        dt_raw = jnp.dot(normed, weight_dt, preferred_element_type=jnp.float32)
        mixer_out, pullback = jax.vjp(mixing, x_raw, bc_raw, dt_raw, conv_inner, conv_shared, head_table)
        gate_act = jax.nn.silu(gate_pre)
        gated_out = mixer_out * gate_act
        scale_gate = lax.rsqrt(lax.optimization_barrier(jnp.mean(gated_out * gated_out, axis=-1, keepdims=True)) + epsilon)
        unit_gate = gated_out * scale_gate
        normed_gate = (unit_gate * gate_gain).astype(jnp.bfloat16)
        rows_out = rows_in + jnp.dot(normed_gate, weight_out.T, preferred_element_type=jnp.float32)
        cot16 = cot_rows.astype(jnp.bfloat16)
        d_gate_out = jnp.dot(cot16, weight_out, preferred_element_type=jnp.float32)
        part_out = jnp.dot(cot16.T, normed_gate, preferred_element_type=jnp.float32)
        part_gate = lax.optimization_barrier(jnp.sum(d_gate_out * unit_gate, axis=0))
        d_unit = d_gate_out * gate_gain
        d_gated = scale_gate * (d_unit - unit_gate * lax.optimization_barrier(jnp.mean(d_unit * unit_gate, axis=-1, keepdims=True)))
        d_mixer = d_gated * gate_act
        sigm = jax.nn.sigmoid(gate_pre)
        d_gate_pre = d_gated * mixer_out * sigm * (1.0 + gate_pre * (1.0 - sigm))
        d_x_raw, d_bc_raw, d_dt_raw, part_conv, part_shared, part_head = pullback(d_mixer)
        d_zx16 = jnp.concatenate([d_gate_pre, d_x_raw], axis=1).astype(jnp.bfloat16)
        d_dt16 = d_dt_raw.astype(jnp.bfloat16)
        d_bc16 = d_bc_raw.astype(jnp.bfloat16)
        d_normed = jnp.dot(d_zx16, flat_zx.T, preferred_element_type=jnp.float32)
        d_normed = d_normed + jnp.dot(d_dt16, weight_dt.T, preferred_element_type=jnp.float32)
        d_normed = d_normed + jnp.dot(d_bc16, weight_bc.T, preferred_element_type=jnp.float32)
        part_zx = jnp.dot(normed.T, d_zx16, preferred_element_type=jnp.float32)
        part_dt = jnp.dot(normed.T, d_dt16, preferred_element_type=jnp.float32)
        part_bc = jnp.dot(normed.T, d_bc16, preferred_element_type=jnp.float32)
        part_norm = lax.optimization_barrier(jnp.sum(d_normed * unit_in, axis=0))
        d_unit_in = d_normed * norm_gain
        rows_grad = cot_rows + scale_in * (d_unit_in - unit_in * lax.optimization_barrier(jnp.mean(d_unit_in * unit_in, axis=-1, keepdims=True)))
        parts = (part_zx, part_dt, part_bc, part_out, part_norm, part_conv, part_shared, part_head, part_gate)
        new_totals = tuple((total + piece for total, piece in zip(totals, parts)))
        return (new_totals, (rows_out, rows_grad))
    start_totals = (jnp.zeros((D, 2 * INNER), jnp.float32), jnp.zeros((D, HEADS), jnp.float32), jnp.zeros((D, 2 * STATE), jnp.float32), jnp.zeros((D, INNER), jnp.float32), jnp.zeros((D,), jnp.float32), jnp.zeros(conv_inner.shape, jnp.float32), jnp.zeros(conv_shared.shape, jnp.float32), jnp.zeros(head_table.shape, jnp.float32), jnp.zeros((INNER,), jnp.float32))
    totals, outputs = lax.scan(one_sequence, start_totals, (hidden_in.reshape(seq_count, LEN, D), cotangent.reshape(seq_count, LEN, D)))
    hidden_out = outputs[0].reshape(hidden_in.shape)
    grad_hidden = outputs[1].reshape(hidden_in.shape)
    grad_zx = totals[0].reshape(D, 2, INNER)
    grads = (grad_zx,) + tuple(totals[1:])
    weights = (proj_zx, proj_dt, proj_bc, proj_out, norm_gain, conv_inner, conv_shared, head_table, gate_gain)
    moments = (mom_zx, mom_dt, mom_bc, mom_out, mom_norm, mom_conv, mom_shared, mom_head, mom_gate)
    seconds = (var_zx, var_dt, var_bc, var_out, var_norm, var_conv, var_shared, var_head, var_gate)
    results = [adam_update(w_item, m_item, v_item, g_item) for w_item, m_item, v_item, g_item in zip(weights, moments, seconds, grads)]
    new_weights = tuple((item[0] for item in results))
    new_moments = tuple((item[1] for item in results))
    new_seconds = tuple((item[2] for item in results))
    return (hidden_out, grad_hidden) + grads + new_weights + new_moments + new_seconds
```

```python
import functools

import jax
import jax.numpy as jnp
from jax import lax
from jax.experimental import pallas as pl
from jax.experimental.pallas import tpu as pltpu
from jax.sharding import PartitionSpec as P

HEAD_DIM = 64
SPAN = 256
LEN = 512
STEP = 3
INNER = 1536


epsilon = 1e-05
precise = lax.Precision.HIGHEST
beta_first = 0.9
beta_second = 0.95
learn_rate = 0.1
weight_decay = 0.01
adam_epsilon = 1e-08


def conv_silu(values, kernel, seq_count):
    kernel_taps = kernel.shape[0] - 1
    shaped = values.reshape(seq_count, LEN, values.shape[1])
    padded = jnp.pad(shaped, ((0, 0), (kernel_taps - 1, 0), (0, 0)))
    summed = kernel[kernel_taps] + jnp.zeros_like(shaped)
    for offset in range(kernel_taps):
        summed = summed + kernel[offset] * padded[:, offset : offset + LEN]
    return jax.nn.silu(summed).reshape(values.shape)


nn_dims = (((1,), (0,)), ((), ()))
nt_dims = (((1,), (1,)), ((), ()))
tn_dims = (((0,), (0,)), ((), ()))
far_below = -1e30


def halves(value):
    high = value.astype(jnp.bfloat16)
    return high, (value - high.astype(jnp.float32)).astype(jnp.bfloat16)


def dot_split(left, right, dims):
    dot = functools.partial(
        lax.dot_general, dimension_numbers=dims, preferred_element_type=jnp.float32
    )
    return dot(left[0], right[0]) + (dot(left[0], right[1]) + dot(left[1], right[0]))


def pick(pair, rows):
    return pair[0][rows], pair[1][rows]


def head_column(table, lane, head):
    return jnp.sum(jnp.where(lane == head, table, 0.0), axis=1, keepdims=True)


def per_lane(columns, width):
    lane = lax.broadcasted_iota(jnp.int32, (1, width), 1)
    result = columns[0]
    for item in range(1, len(columns)):
        result = jnp.where(lane >= item * HEAD_DIM, columns[item], result)
    return jnp.broadcast_to(result, (columns[0].shape[0], width))


def in_head(width, item):
    lane = lax.broadcasted_iota(jnp.int32, (1, width), 1)
    return (lane >= item * HEAD_DIM) & (lane < (item + 1) * HEAD_DIM)


def forward_kernel(group, u_ref, dt_ref, cum_ref, row_ref, bc_ref, skip_ref, y_ref, scores):
    step = pl.program_id(1)
    width = u_ref.shape[1]
    state_dim = bc_ref.shape[1] // 2

    @pl.when(step == 0)
    def _():
        keys, queries = halves(bc_ref[:, :state_dim]), halves(bc_ref[:, state_dim:])
        scores[...] = dot_split(queries, keys, nt_dims)

    lane = lax.broadcasted_iota(jnp.int32, dt_ref.shape, 1)
    dts = [head_column(dt_ref[...], lane, step * group + item) for item in range(group)]
    cums = [head_column(cum_ref[...], lane, step * group + item) for item in range(group)]
    weighted = halves(u_ref[...] * per_lane(dts, width))
    for block in range(LEN // SPAN):
        rows = slice(block * SPAN, (block + 1) * SPAN)
        past = slice(0, (block + 1) * SPAN)
        shape = (SPAN, (block + 1) * SPAN)
        mask = (
            lax.broadcasted_iota(jnp.int32, shape, 0) + block * SPAN
            >= lax.broadcasted_iota(jnp.int32, shape, 1)
        )
        total = skip_ref[...] * u_ref[rows, :]
        for item in range(group):
            row = row_ref[0, pl.ds(step * group + item, 1), past]
            decay = jnp.exp(jnp.where(mask, cums[item][rows] - row, far_below))
            mixing_table = halves(scores[rows, past] * decay)
            part = dot_split(mixing_table, pick(weighted, past), nn_dims)
            total = total + jnp.where(in_head(width, item), part, 0.0)
        y_ref[rows, :] = total


def backward_kernel(
    group,
    dy_ref,
    y_ref,
    u_ref,
    dt_ref,
    cum_ref,
    row_ref,
    bc_ref,
    skip_ref,
    du_ref,
    ddt_ref,
    dcum_ref,
    dskip_ref,
    dbc_ref,
    scores,
    d_scores,
):
    step = pl.program_id(1)
    width = u_ref.shape[1]
    state_dim = bc_ref.shape[1] // 2

    @pl.when(step == 0)
    def _():
        keys, queries = halves(bc_ref[:, :state_dim]), halves(bc_ref[:, state_dim:])
        scores[...] = dot_split(keys, queries, nt_dims)
        d_scores[...] = jnp.zeros_like(d_scores)
        ddt_ref[...] = jnp.zeros_like(ddt_ref)
        dcum_ref[...] = jnp.zeros_like(dcum_ref)
        dskip_ref[...] = jnp.zeros_like(dskip_ref)

    lane = lax.broadcasted_iota(jnp.int32, dt_ref.shape, 1)
    dts = [head_column(dt_ref[...], lane, step * group + item) for item in range(group)]
    cums = [head_column(cum_ref[...], lane, step * group + item) for item in range(group)]
    dt_lanes = per_lane(dts, width)
    weighted = u_ref[...] * dt_lanes
    split_w = halves(weighted)
    split_dy = halves(dy_ref[...])
    for block in range(LEN // SPAN):
        rows = slice(block * SPAN, (block + 1) * SPAN)
        later = slice(block * SPAN, LEN)
        shape = (SPAN, LEN - block * SPAN)
        mask = lax.broadcasted_iota(jnp.int32, shape, 0) <= lax.broadcasted_iota(
            jnp.int32, shape, 1
        )
        dy_later = pick(split_dy, later)
        dw = jnp.zeros((SPAN, width), jnp.float32)
        d_block = jnp.zeros(shape, jnp.float32)
        for item in range(group):
            inside = in_head(width, item)
            row = row_ref[0, pl.ds(step * group + item, 1), later]
            decay = jnp.exp(jnp.where(mask, row - cums[item][rows], far_below))
            mixing_table = halves(scores[rows, later] * decay)
            part = dot_split(mixing_table, dy_later, nn_dims)
            dw = dw + jnp.where(inside, part, 0.0)
            own = halves(jnp.where(inside, weighted[rows], 0.0))
            d_block = d_block + dot_split(own, dy_later, nt_dims) * decay
        d_scores[rows, later] += d_block
        u = u_ref[rows, :]
        dy = dy_ref[rows, :]
        du_ref[rows, :] = dw * dt_lanes[rows] + skip_ref[...] * dy
        dw_u = dw * u
        dy_u = dy * u
        balance = dy * (y_ref[rows, :] - skip_ref[...] * u) - weighted[rows] * dw
        for item in range(group):
            inside = in_head(width, item)
            here = lane[rows] == step * group + item
            for ref, value in ((ddt_ref, dw_u), (dcum_ref, balance), (dskip_ref, dy_u)):
                column = jnp.sum(jnp.where(inside, value, 0.0), axis=1, keepdims=True)
                ref[rows, :] += jnp.where(here, column, 0.0)

    @pl.when(step == pl.num_programs(1) - 1)
    def _():
        keys, queries = halves(bc_ref[:, :state_dim]), halves(bc_ref[:, state_dim:])
        split_d = halves(d_scores[...])
        dbc_ref[:, :state_dim] = dot_split(split_d, queries, nn_dims)
        dbc_ref[:, state_dim:] = dot_split(split_d, keys, tn_dims)


def mixer_specs(heads, inner):
    group = 2 if heads % 2 == 0 else heads
    width = inner * group // heads
    wide = pl.BlockSpec((LEN, width), lambda seq, step: (seq, step))
    table = pl.BlockSpec((LEN, heads), lambda seq, step: (seq, 0))
    lines = pl.BlockSpec((1, heads, LEN), lambda seq, step: (seq, 0, 0))
    skip = pl.BlockSpec((1, width), lambda seq, step: (0, step))
    return group, wide, table, lines, skip


def mixer_forward(u, step_size, cum, cum_rows, bc_conv, skip_lanes):
    tokens, inner = u.shape
    heads = step_size.shape[1]
    group, wide, table, lines, skip = mixer_specs(heads, inner)
    shared = pl.BlockSpec((LEN, bc_conv.shape[1]), lambda seq, step: (seq, 0))
    return pl.pallas_call(
        functools.partial(forward_kernel, group),
        out_shape=jax.ShapeDtypeStruct(u.shape, jnp.float32),
        grid=(tokens // LEN, heads // group),
        in_specs=[wide, table, table, lines, shared, skip],
        out_specs=wide,
        scratch_shapes=[pltpu.VMEM((LEN, LEN), jnp.float32)],
        name="mixer_forward",
    )(u, step_size, cum, cum_rows, bc_conv, skip_lanes)


def mixer_backward(dy, y, u, step_size, cum, cum_rows, bc_conv, skip_lanes):
    tokens, inner = u.shape
    heads = step_size.shape[1]
    group, wide, table, lines, skip = mixer_specs(heads, inner)
    shared = pl.BlockSpec((LEN, bc_conv.shape[1]), lambda seq, step: (seq, 0))
    small = jax.ShapeDtypeStruct(step_size.shape, jnp.float32)
    return pl.pallas_call(
        functools.partial(backward_kernel, group),
        out_shape=(
            jax.ShapeDtypeStruct(u.shape, jnp.float32),
            small,
            small,
            small,
            jax.ShapeDtypeStruct(bc_conv.shape, jnp.float32),
        ),
        grid=(tokens // LEN, heads // group),
        in_specs=[wide, wide, wide, table, table, lines, shared, skip],
        out_specs=(wide, table, table, table, shared),
        scratch_shapes=[pltpu.VMEM((LEN, LEN), jnp.float32)] * 2,
        name="mixer_backward",
    )(dy, y, u, step_size, cum, cum_rows, bc_conv, skip_lanes)


def shift(value, axis, count, offset):
    return lax.ppermute(value, axis, [(i, (i + offset) % count) for i in range(count)])


def gather_rows(value, axis):
    count, me = lax.axis_size(axis), lax.axis_index(axis)
    rows = value.shape[0]
    whole = jnp.zeros((count * rows,) + value.shape[1:], value.dtype)
    for offset in range(count):
        piece = shift(value, axis, count, offset) if offset else value
        source = lax.rem(me + count - offset, count)
        whole = lax.dynamic_update_slice_in_dim(whole, piece, source * rows, 0)
    return whole


def scatter_rows(value, axis, kind):
    count, me = lax.axis_size(axis), lax.axis_index(axis)
    rows = value.shape[0] // count
    total = lax.dynamic_slice_in_dim(value, me * rows, rows, 0)
    for offset in range(1, count):
        target = lax.rem(me + offset, count)
        piece = lax.dynamic_slice_in_dim(value, target * rows, rows, 0).astype(kind)
        total = total + shift(piece, axis, count, offset).astype(jnp.float32)
    return total


def butterfly_ok(axis):
    count = lax.axis_size(axis)
    return count & (count - 1) == 0


def flip(value, axis, bit):
    count = lax.axis_size(axis)
    return lax.ppermute(value, axis, [(i, i ^ bit) for i in range(count)])


def sum_all(value, axis):
    if not butterfly_ok(axis):
        return lax.psum(value, axis)
    bit = 1
    while bit < lax.axis_size(axis):
        value = value + flip(value, axis, bit)
        bit *= 2
    return value


def scatter_halving(value, axis):
    if not butterfly_ok(axis):
        return lax.psum_scatter(value, axis, scatter_dimension=0, tiled=True)
    count, me = lax.axis_size(axis), lax.axis_index(axis)
    rows = value.shape[0] // count
    tail = value.shape[1:]
    bit = 1
    while bit < count:
        count_left = count // (2 * bit)
        value = value.reshape((count_left, 2, rows) + tail)
        mine = lax.rem(me // bit, 2)
        keep = lax.dynamic_index_in_dim(value, mine, 1, keepdims=False)
        give = lax.dynamic_index_in_dim(value, 1 - mine, 1, keepdims=False)
        moved = flip(give, axis, bit)
        value = keep + moved
        bit *= 2
    return value.reshape((rows,) + tail)


def adam_update(weight, moment, second, gradient):
    moment_new = beta_first * moment + (1.0 - beta_first) * gradient
    second_new = beta_second * second + (1.0 - beta_second) * gradient * gradient
    corr_first = 1.0 - beta_first**STEP
    corr_second = 1.0 - beta_second**STEP
    update = moment_new / corr_first / (jnp.sqrt(second_new / corr_second) + adam_epsilon)
    return (weight - learn_rate * (update + weight_decay * weight), moment_new, second_new)


def whole_step(
    hidden_in,
    cotangent,
    proj_zx,
    proj_dt,
    proj_bc,
    proj_out,
    norm_gain,
    conv_inner,
    conv_shared,
    head_table,
    gate_gain,
    mom_zx,
    mom_dt,
    mom_bc,
    mom_out,
    mom_norm,
    mom_conv,
    mom_shared,
    mom_head,
    mom_gate,
    var_zx,
    var_dt,
    var_bc,
    var_out,
    var_norm,
    var_conv,
    var_shared,
    var_head,
    var_gate,
):
    inner_local = proj_out.shape[1]
    heads_local = proj_dt.shape[1]
    shard_rows = proj_zx.shape[0]
    columns = (2 * inner_local, proj_bc.shape[1], heads_local)
    cot_all = gather_rows(cotangent.astype(jnp.bfloat16), "tensor")
    scale_in = lax.rsqrt(jnp.mean(hidden_in * hidden_in, axis=-1, keepdims=True) + epsilon)
    unit_in = hidden_in * scale_in
    normed_local = (unit_in * norm_gain).astype(jnp.bfloat16)
    normed = gather_rows(normed_local, "tensor")
    packed = jnp.concatenate(
        [proj_zx.reshape(shard_rows, columns[0]), proj_out, proj_bc, proj_dt], axis=1
    ).astype(jnp.bfloat16)
    full_in = lax.all_gather(packed, "dp", axis=0, tiled=True)
    full_z = full_in[:, :inner_local]
    full_x = full_in[:, inner_local : columns[0]]
    bc_start = columns[0] + inner_local
    full_out = full_in[:, columns[0] : bc_start]
    full_bc = full_in[:, bc_start : bc_start + columns[1]]
    full_dt = full_in[:, bc_start + columns[1] :]
    seq_count = normed.shape[0] // LEN
    x_raw = jnp.dot(normed, full_x, preferred_element_type=jnp.float32)
    bc_raw = jnp.dot(normed, full_bc, preferred_element_type=jnp.float32)
    dt_raw = jnp.dot(normed, full_dt, preferred_element_type=jnp.float32)
    gate_pre = jnp.dot(normed, full_z, preferred_element_type=jnp.float32)
    x_conv, pull_inner = jax.vjp(lambda v, k: conv_silu(v, k, seq_count), x_raw, conv_inner)
    bc_conv, pull_shared = jax.vjp(lambda v, k: conv_silu(v, k, seq_count), bc_raw, conv_shared)
    dt_pre = dt_raw + head_table[0]
    step_size = jax.nn.softplus(dt_pre)
    decay_rate = -jnp.exp(head_table[1])
    position = jnp.arange(LEN)
    lower = (position[:, None] >= position[None, :]).astype(jnp.float32)
    rates = (step_size * decay_rate).reshape(seq_count, LEN, heads_local)
    cum = jnp.einsum("ts,bsh->bth", lower, rates, precision=precise)
    cum_rows = jnp.swapaxes(cum, 1, 2)
    cum = cum.reshape(step_size.shape)
    skip_lanes = jnp.repeat(head_table[2], HEAD_DIM)[None]
    mixer_out = mixer_forward(x_conv, step_size, cum, cum_rows, bc_conv, skip_lanes)
    gate_act = jax.nn.silu(gate_pre)
    gated_out = mixer_out * gate_act
    d_gate_out = jnp.dot(cot_all, full_out, preferred_element_type=jnp.float32)
    d_unit = d_gate_out * gate_gain
    square_sum, gated_dot = sum_all(
        jnp.stack(
            [jnp.sum(gated_out * gated_out, axis=-1), jnp.sum(d_unit * gated_out, axis=-1)]
        ),
        "tensor",
    )
    scale_gate = lax.rsqrt(square_sum / INNER + epsilon)[:, None]
    unit_gate = gated_out * scale_gate
    normed_gate = (unit_gate * gate_gain).astype(jnp.bfloat16)
    inner_dot = gated_dot * scale_gate[:, 0]
    grad_out_group = jnp.dot(cot_all.T, normed_gate, preferred_element_type=jnp.float32)
    grad_out = scatter_halving(grad_out_group, "dp")
    branch_full = jnp.dot(normed_gate, full_out.T, preferred_element_type=jnp.float32)
    branch_out = scatter_rows(branch_full, "tensor", jnp.bfloat16)
    hidden_out = hidden_in + branch_out
    gate_part = jnp.sum(d_gate_out * unit_gate, axis=0)
    d_gated = scale_gate * (d_unit - unit_gate * (inner_dot / INNER)[:, None])
    d_mixer = d_gated * gate_act
    sigm = jax.nn.sigmoid(gate_pre)
    d_z16 = (d_gated * mixer_out * sigm * (1.0 + gate_pre * (1.0 - sigm))).astype(jnp.bfloat16)
    z_group = jnp.dot(normed.T, d_z16, preferred_element_type=jnp.float32)
    grad_z = scatter_halving(z_group, "dp")
    d_conv, d_step, d_cum, d_skip, d_bc_conv = mixer_backward(
        d_mixer, mixer_out, x_conv, step_size, cum, cum_rows, bc_conv, skip_lanes
    )
    d_bc_part, shared_part = pull_shared(d_bc_conv)
    own_bc = scatter_rows(d_bc_part, "tensor", jnp.float32).astype(jnp.bfloat16)
    d_x_raw, conv_part = pull_inner(d_conv)
    d_rates = jnp.einsum(
        "ts,bth->bsh", lower, d_cum.reshape(rates.shape), precision=precise
    ).reshape(step_size.shape)
    d_dt_raw = (d_step + d_rates * decay_rate) * jax.nn.sigmoid(dt_pre)
    head_part = jnp.stack(
        [
            jnp.sum(d_dt_raw, axis=0),
            jnp.sum(d_rates * step_size, axis=0) * decay_rate,
            jnp.sum(d_skip, axis=0),
        ]
    )
    d_x16 = d_x_raw.astype(jnp.bfloat16)
    d_dt16 = d_dt_raw.astype(jnp.bfloat16)
    x_group = jnp.dot(normed.T, d_x16, preferred_element_type=jnp.float32)
    grad_x = scatter_halving(x_group, "dp")
    dt_group = jnp.dot(normed.T, d_dt16, preferred_element_type=jnp.float32)
    bc_own = jnp.dot(normed_local.T, own_bc, preferred_element_type=jnp.float32)
    partial_in = jnp.dot(d_z16, full_z.T, preferred_element_type=jnp.float32)
    partial_in = partial_in + jnp.dot(d_x16, full_x.T, preferred_element_type=jnp.float32)
    partial_in = partial_in + jnp.dot(d_dt16, full_dt.T, preferred_element_type=jnp.float32)
    d_normed = scatter_rows(partial_in, "tensor", jnp.bfloat16)
    d_normed = d_normed + jnp.dot(own_bc, full_bc.T, preferred_element_type=jnp.float32)
    norm_part = jnp.sum(d_normed * unit_in, axis=0)
    d_unit_in = d_normed * norm_gain
    grad_hidden = cotangent + scale_in * (
        d_unit_in - unit_in * jnp.mean(d_unit_in * unit_in, axis=-1, keepdims=True)
    )
    side = scatter_halving(jnp.concatenate([bc_own, dt_group], axis=1), "dp")
    grad_bc = sum_all(side[:, : columns[1]], "tensor")
    grad_dt = side[:, columns[1] :]
    grad_zx = jnp.stack([grad_z, grad_x], axis=1)
    parts = (conv_part, gate_part, head_part, shared_part, norm_part)
    flat = sum_all(jnp.concatenate([part.reshape(-1) for part in parts]), "dp")
    sums = []
    offset = 0
    for part in parts:
        sums.append(flat[offset : offset + part.size].reshape(part.shape))
        offset += part.size
    grad_conv, grad_gate, grad_head = sums[:3]
    both = sum_all(jnp.concatenate([sums[3].reshape(-1), sums[4]]), "tensor")
    sum_shared = both[: shared_part.size].reshape(shared_part.shape)
    sum_norm = both[shared_part.size :]
    grads = (
        grad_zx,
        grad_dt,
        grad_bc,
        grad_out,
        sum_norm,
        grad_conv,
        sum_shared,
        grad_head,
        grad_gate,
    )
    weights = (
        proj_zx,
        proj_dt,
        proj_bc,
        proj_out,
        norm_gain,
        conv_inner,
        conv_shared,
        head_table,
        gate_gain,
    )
    moments = (mom_zx, mom_dt, mom_bc, mom_out, mom_norm, mom_conv, mom_shared, mom_head, mom_gate)
    seconds = (var_zx, var_dt, var_bc, var_out, var_norm, var_conv, var_shared, var_head, var_gate)
    results = [
        adam_update(w_item, m_item, v_item, g_item)
        for w_item, m_item, v_item, g_item in zip(weights, moments, seconds, grads)
    ]
    new_weights = tuple((item[0] for item in results))
    new_moments = tuple((item[1] for item in results))
    new_seconds = tuple((item[2] for item in results))
    return (hidden_out, grad_hidden) + grads + new_weights + new_moments + new_seconds


def solution(mesh):
    placed = (
        P(("dp", "tensor"), None),
        P(("dp", "tensor"), None),
        P("dp", None, "tensor"),
        P("dp", "tensor"),
        P("dp", None),
        P("dp", "tensor"),
        P(),
        P(None, "tensor"),
        P(),
        P(None, "tensor"),
        P("tensor"),
        P("dp", None, "tensor"),
        P("dp", "tensor"),
        P("dp", None),
        P("dp", "tensor"),
        P(),
        P(None, "tensor"),
        P(),
        P(None, "tensor"),
        P("tensor"),
        P("dp", None, "tensor"),
        P("dp", "tensor"),
        P("dp", None),
        P("dp", "tensor"),
        P(),
        P(None, "tensor"),
        P(),
        P(None, "tensor"),
        P("tensor"),
    )
    return jax.shard_map(
        whole_step,
        mesh=mesh,
        in_specs=placed,
        out_specs=(
            P(("dp", "tensor"), None),
            P(("dp", "tensor"), None),
            P("dp", None, "tensor"),
            P("dp", "tensor"),
            P("dp", None),
            P("dp", "tensor"),
            P(),
            P(None, "tensor"),
            P(),
            P(None, "tensor"),
            P("tensor"),
            P("dp", None, "tensor"),
            P("dp", "tensor"),
            P("dp", None),
            P("dp", "tensor"),
            P(),
            P(None, "tensor"),
            P(),
            P(None, "tensor"),
            P("tensor"),
            P("dp", None, "tensor"),
            P("dp", "tensor"),
            P("dp", None),
            P("dp", "tensor"),
            P(),
            P(None, "tensor"),
            P(),
            P(None, "tensor"),
            P("tensor"),
            P("dp", None, "tensor"),
            P("dp", "tensor"),
            P("dp", None),
            P("dp", "tensor"),
            P(),
            P(None, "tensor"),
            P(),
            P(None, "tensor"),
            P("tensor"),
        ),
        check_vma=False,
    )
```
